32 devices in a mesh: groups: 2 (over x), gx: 8 (over z, y), shot: 2 (over core).
Axes of the slice: x: 2, y: 2, z: 4, core: 2. Of those that a mesh axis runs over, the one named last changes fastest.
Arguments:
- src_now: float32 [8, 128, 64, 128], P(('groups', 'shot'), 'gx'), parts along dimension 0, may hold values from -6 to 6
- src_prev: float32 [8, 128, 64, 128], P(('groups', 'shot'), 'gx'), parts along dimension 0, may hold values from -6 to 6
- rec_now: float32 [8, 128, 64, 128], P(('groups', 'shot'), 'gx'), parts along dimension 0, may hold values from -6 to 6
- rec_prev: float32 [8, 128, 64, 128], P(('groups', 'shot'), 'gx'), parts along dimension 0, may hold values from -6 to 6
- courant_sq: float32 [256, 64, 128], P(('groups', 'gx')), parts along dimension 0, may hold values from 0.05 to 0.3
- wavelet: float32 [8, 4], P(('groups', 'shot')), parts along dimension 0, may hold values from -8 to 8
- traces: float32 [8, 4, 128], P(('groups', 'shot'), None, 'gx'), parts along dimension 0, may hold values from -6 to 6
- positions: int32 [8, 4], P(('groups', 'shot')), parts along dimension 0, may hold values from 0 to 127, as said below
Outputs:
- angle_image: float32 [16, 128, 32, 128], P(('groups', 'shot'), 'gx'), parts along dimension 0
The draws below stay inside these ranges and needn't reach their ends.
There are 2 independent parts, one for each index of `groups`. The reference program is written for one: setup_inputs(seed, part) draws one part's arguments, and reference() takes and returns one part's arrays. A program takes and returns all parts, laid end to end along the dimension named above; each array names one. Nothing has to cross between parts.
Inputs may be any that keep to these rules, and one draw needn't show every extreme that they name: `positions`: column 0 lies in 0 .. 127, columns 1 and 3 in 0 .. 127, column 2 in 0 .. 63; one shot of each patch has its source at x 128 - 1, y * 128 - 1, depth 64 - 1 and its receiver line at y 0.
All inputs are finite; a program needn't handle non-finite values.
Results may differ from the reference program's by a relative error of at most 0.0001.
Values sent between devices are 32-bit elements; how exact they have to be, the bound alone decides.
A program may use at most 192 MiB of HBM per device.

```python
import math
import jax
import jax.numpy as jnp
from jax import lax

NY = 128
NZ = 64
STEPS = 4
IMAGES = 2
LAGS = 49
ANGLES = 8
HALF = 24
NZH = 32
NX = 128
SHOTS = 4


def draw_positions(key, part):
    limits = jnp.array([NX, NY, NZ, NY], jnp.int32)
    raw = jax.random.randint(jax.random.fold_in(key, 7), (SHOTS, 4), 0, 1 << 20, dtype=jnp.int32)
    drawn = raw % limits[None, :]
    corner = jnp.array([NX - 1, NY - 1, NZ - 1, 0], jnp.int32)
    return drawn.at[0].set(corner)


def block_scale(rng, dims, cuts, least, top_value):
    gain = 1.0
    for axis_at, blocks in cuts:
        steps = jax.random.uniform(jax.random.fold_in(jax.random.fold_in(rng, 6), axis_at), (blocks,), jnp.float32, least / len(cuts), top_value / len(cuts))
        gain = gain * jnp.repeat(jnp.exp(steps), dims[axis_at] // blocks).reshape((-1,) + (1,) * (len(dims) - 1 - axis_at))
    return gain


def gaussian(key, shape, scale, reach, pieces=(), kind=jnp.bfloat16):
    entries = scale * jax.random.normal(key, shape, jnp.float32)
    if pieces:
        entries = entries * block_scale(key, shape, pieces, -0.22, 0.18)
    return jnp.clip(entries, -reach, reach).astype(kind)


def setup_inputs(seed: int = 0, part: int = 0) -> dict:
    seeds = jax.random.split(jax.random.key(seed), 9)
    part_keys = jax.random.split(jax.random.fold_in(seeds[8], part), 9)
    return {
        "src_now": gaussian(part_keys[0], (SHOTS, NX, NZ, NY), 1.0, 6.0, ((0, 2), (1, 8)), jnp.float32),
        "src_prev": gaussian(part_keys[1], (SHOTS, NX, NZ, NY), 1.0, 6.0, ((0, 2), (1, 8)), jnp.float32),
        "rec_now": gaussian(part_keys[2], (SHOTS, NX, NZ, NY), 1.0, 6.0, ((0, 2), (1, 8)), jnp.float32),
        "rec_prev": gaussian(part_keys[3], (SHOTS, NX, NZ, NY), 1.0, 6.0, ((0, 2), (1, 8)), jnp.float32),
        "courant_sq": jnp.clip(jnp.exp(math.log(0.3) - 1.7917595 * jax.random.uniform(part_keys[4], (NX, NZ, NY), jnp.float32) ** block_scale(part_keys[4], (NX, NZ, NY), ((0, 8),), -0.2, 0.2)), 0.05, 0.3),
        "wavelet": gaussian(part_keys[5], (SHOTS, STEPS), 2.0, 8.0, ((0, 2),), jnp.float32),
        "traces": gaussian(part_keys[6], (SHOTS, STEPS, NX), 1.0, 6.0, ((0, 2), (2, 8)), jnp.float32),
        "positions": draw_positions(jax.random.fold_in(jax.random.fold_in(seeds[8], part), 71), part),
    }


def laplace(field):
    padded = jnp.pad(field, ((0, 0), (1, 1), (1, 1), (1, 1)))
    beside = padded[:, 2:, 1:-1, 1:-1] + padded[:, :-2, 1:-1, 1:-1]
    beside = beside + padded[:, 1:-1, 2:, 1:-1] + padded[:, 1:-1, :-2, 1:-1]
    beside = beside + padded[:, 1:-1, 1:-1, 2:] + padded[:, 1:-1, 1:-1, :-2]
    return beside - 6.0 * field

def slant_stack(source, receiver):
    width = source.shape[1]
    spad = jnp.pad(source, ((0, 0), (HALF, HALF), (0, 0), (0, 0)))
    rpad = jnp.pad(receiver, ((0, 0), (HALF, HALF), (0, 0), (0, 0)))
    totals = [None] * ANGLES
    for index in range(LAGS):
        offset = index - HALF
        product = lax.optimization_barrier(jnp.sum(spad[:, HALF - offset:HALF - offset + width] * rpad[:, HALF + offset:HALF + offset + width], axis=0))
        for angle in range(ANGLES):
            moved = angle * abs(offset) // ANGLES
            piece = product[:, moved:moved + NZH, :]
            totals[angle] = piece if totals[angle] is None else totals[angle] + piece
    return jnp.stack(totals)

def reference(src_now, src_prev, rec_now, rec_prev, courant_sq, wavelet, traces, positions):
    ftype = src_now.dtype
    xgrid = jnp.arange(NX, dtype=jnp.int32)
    ygrid = jnp.arange(NY, dtype=jnp.int32)
    zgrid = jnp.arange(NZ, dtype=jnp.int32)
    source_mask = ((xgrid[None, :, None, None] == positions[:, 0, None, None, None]) & (zgrid[None, None, :, None] == positions[:, 2, None, None, None]) & (ygrid[None, None, None, :] == positions[:, 1, None, None, None])).astype(ftype)
    line_mask = (ygrid[None, :] == positions[:, 3, None]).astype(ftype)
    every = STEPS // IMAGES
    total = jnp.zeros((ANGLES, NX, NZH, NY), ftype)
    for step in range(STEPS):
        src_next = 2.0 * src_now - src_prev + courant_sq[None] * laplace(src_now) + wavelet[:, step, None, None, None] * source_mask
        rec_next = 2.0 * rec_now - rec_prev + courant_sq[None] * laplace(rec_now)
        rec_next = rec_next.at[:, :, 0, :].add(traces[:, STEPS - 1 - step, :, None] * line_mask[:, None, :])
        src_prev, src_now = (src_now, src_next)
        rec_prev, rec_now = (rec_now, rec_next)
        if (step + 1) % every == 0:
            total = total + slant_stack(src_now, rec_now)
    return total * (1.0 / math.sqrt(LAGS * SHOTS * IMAGES))
```

```python
import functools
import math

import jax
import jax.numpy as jnp
from jax import lax
from jax.experimental import pallas as pl
from jax.experimental.pallas import tpu as pltpu
from jax.sharding import PartitionSpec as P

STEPS = 4
IMAGES = 2
LAGS = 49
ANGLES = 8
HALF = (LAGS - 1) // 2
MESH = pl.DeviceIdType.MESH


def kernel(
    n,
    scale,
    rows,
    positions,
    wavelet,
    traces,
    src_now,
    src_prev,
    rec_now,
    rec_prev,
    courant_hbm,
    out,
    level,
    courant,
    window,
    image,
    from_core,
    summed,
    from_pair,
    product,
    load_sem,
    halo_send,
    halo_recv,
    pair_send,
    pair_recv,
    up_send,
    up_recv,
    down_send,
    down_recv,
    core_send,
    core_recv,
    out_send,
    out_recv,
):
    planes, depth, width = courant.shape
    block = planes // 2
    shots = src_now.shape[0]
    angles_out, _, depth_out, _ = out.shape
    me = lax.axis_index("gx")
    core = lax.axis_index("shot")
    y = lax.rem(me, 2)
    pair = me + 1 - 2 * y
    other = 1 - core
    has_below = me >= 2
    has_above = me < n - 2

    loads = []
    for i, (ref, k, f) in enumerate(
        ((src_now, 1, 0), (rec_now, 1, 1), (src_prev, 0, 0), (rec_prev, 0, 1))
    ):
        loads.append(
            pltpu.make_async_copy(ref, level.at[k, f, :, pl.ds(1, planes)], load_sem.at[i])
        )
    loads.append(pltpu.make_async_copy(courant_hbm, courant, load_sem.at[4]))
    for load in loads:
        load.start()

    barrier = pltpu.get_barrier_semaphore()
    for step in (-2, -1, 1, 2):
        there = me + step

        @pl.when((there >= 0) & (there < n))
        def _():
            pl.semaphore_signal(barrier, inc=1, device_id={"gx": there}, device_id_type=MESH)

    pl.semaphore_signal(barrier, inc=1, device_id={"shot": other}, device_id_type=MESH)

    edge = jnp.zeros((rows, width), jnp.float32)
    full = jnp.zeros((depth, width), jnp.float32)

    @pl.when(me == 0)
    def _():
        for k in range(1, STEPS + 1):
            for f in range(2):
                for s in range(shots):
                    level[k, f, s, 0] = full

    @pl.when(me == n - 1)
    def _():
        for k in range(1, STEPS + 1):
            for f in range(2):
                for s in range(shots):
                    level[k, f, s, planes + 1] = full

    @pl.when(jnp.logical_not(has_below))
    def _():
        @pl.loop(0, HALF)
        def _(q):
            for g in range(IMAGES):
                for f in range(2):
                    window[g, f, q] = edge

    @pl.when(jnp.logical_not(has_above))
    def _():
        @pl.loop(0, HALF)
        def _(q):
            for g in range(IMAGES):
                for f in range(2):
                    window[g, f, HALF + 2 * planes + q] = edge

    peers = jnp.minimum(me, 2) + jnp.minimum(n - 1 - me, 2) + 1
    pl.semaphore_wait(barrier, peers)

    def halo(t, side):
        height = depth if t == 0 else rows
        kept = pl.ds(0, height)
        source, target = (planes, 0) if side == 0 else (1, planes + 1)
        return pltpu.make_async_remote_copy(
            src_ref=level.at[1 + t, :, :, source, kept],
            dst_ref=level.at[1 + t, :, :, target, kept],
            send_sem=halo_send.at[t, side],
            recv_sem=halo_recv.at[t, side],
            device_id={"gx": me + 1 if side == 0 else me - 1},
            device_id_type=MESH,
        )

    def send_halo(t):
        @pl.when(me < n - 1)
        def _():
            halo(t, 0).start()

        @pl.when(me > 0)
        def _():
            halo(t, 1).start()

    def wait_halo(t):
        @pl.when(me > 0)
        def _():
            halo(t, 0).wait_recv()

        @pl.when(me < n - 1)
        def _():
            halo(t, 1).wait_recv()

    z_row = lax.broadcasted_iota(jnp.int32, (rows, width), 0)
    y_lane = lax.broadcasted_iota(jnp.int32, (rows, width), 1)
    first = me * planes

    def plane_step(t, x):
        speed = courant[x - 1, :rows]
        tall = depth if t == 0 else rows
        for s in range(shots):
            for f in range(2):
                now_tall = level[1 + t, f, s, x, :tall]
                now = now_tall[:rows]
                low = level[1 + t, f, s, x - 1, :rows]
                high = level[1 + t, f, s, x + 1, :rows]
                zeros = jnp.zeros((1, width), jnp.float32)
                deeper = jnp.concatenate([now_tall[1:], zeros], axis=0)[:rows]
                shallower = jnp.concatenate([zeros, now[: rows - 1]], axis=0)
                left = jnp.where(y_lane == 0, 0.0, pltpu.roll(now, 1, 1))
                right = jnp.where(y_lane == width - 1, 0.0, pltpu.roll(now, width - 1, 1))
                beside = low + high + deeper + shallower + left + right
                nxt = 2.0 * now - level[t, f, s, x, :rows] + speed * (beside - 6.0 * now)
                if f == 0:
                    amount = jnp.where(first + x - 1 == positions[s, 0], wavelet[s, t], 0.0)
                    hit = (z_row == positions[s, 2]) & (y_lane == positions[s, 1])
                else:
                    amount = traces[s, STEPS - 1 - t, x - 1]
                    hit = (z_row == 0) & (y_lane == positions[s, 3])
                level[2 + t, f, s, x, :rows] = nxt + jnp.where(hit, amount, 0.0)

    def wave_step(t):
        @pl.loop(2, planes)
        def _(x):
            plane_step(t, x)

        wait_halo(t)
        for half in range(2):
            @pl.loop(0, 1)
            def _(_i, half=half):
                plane_step(t, 1 + half * (planes - 1))

    def pair_copy(g, part):
        at = block * (1 - y) if part == 0 else block * y
        return pltpu.make_async_remote_copy(
            src_ref=level.at[2 * g + 3, :, 1 - y, pl.ds(1 + at, block), pl.ds(0, rows)],
            dst_ref=window.at[g, :, pl.ds(HALF + planes * y + at, block)],
            send_sem=pair_send.at[g, part],
            recv_sem=pair_recv.at[g, part],
            device_id={"gx": pair},
            device_id_type=MESH,
        )

    def up_copy(g, k):
        return pltpu.make_async_remote_copy(
            src_ref=window.at[g, :, pl.ds(HALF + block * (k + 1), block)],
            dst_ref=window.at[g, :, pl.ds(block * k, block)],
            send_sem=up_send.at[g, k],
            recv_sem=up_recv.at[g, k],
            device_id={"gx": me + 2},
            device_id_type=MESH,
        )

    def down_copy(g, k):
        return pltpu.make_async_remote_copy(
            src_ref=window.at[g, :, pl.ds(HALF + block * k, block)],
            dst_ref=window.at[g, :, pl.ds(HALF + 2 * planes + block * k, block)],
            send_sem=down_send.at[g, k],
            recv_sem=down_recv.at[g, k],
            device_id={"gx": me - 2},
            device_id_type=MESH,
        )

    def send_inner(g, owner):
        @pl.when(has_above)
        def _():
            up_copy(g, owner).start()

        @pl.when(has_below)
        def _():
            down_copy(g, 1 + owner).start()

    def send_outer(g, owner):
        @pl.when(has_above & (owner == 1))
        def _():
            up_copy(g, 2).start()

        @pl.when(has_below & (owner == 0))
        def _():
            down_copy(g, 0).start()

    def own_out(g):
        pair_copy(g, 0).start()
        pair_copy(g, 1).start()

        @pl.loop(0, planes)
        def _(x):
            for f in range(2):
                window[g, f, HALF + planes * y + x] = level[2 * g + 3, f, y, 1 + x, :rows]

        send_inner(g, y)
        send_outer(g, y)

    def relay(g):
        pair_copy(g, 0).wait_recv()
        send_inner(g, 1 - y)
        pair_copy(g, 1).wait_recv()
        send_outer(g, 1 - y)

    def wait_window(g):
        for k in range(3):
            @pl.when(has_below)
            def _():
                up_copy(g, k).wait_recv()

            @pl.when(has_above)
            def _():
                down_copy(g, k).wait_recv()

    def image_chunk(g, chunk):
        @pl.loop(0, block)
        def _(x):
            at = HALF + chunk * block + x
            totals = [None] * ANGLES
            for h in range(HALF + 1):
                reach = depth_out + (ANGLES - 1) * h // ANGLES
                tall = min(rows, -(-reach // 8) * 8)
                value = window[g, 0, at - h, :tall] * window[g, 1, at + h, :tall]
                if h:
                    value = value + window[g, 0, at + h, :tall] * window[g, 1, at - h, :tall]
                if h > 1:
                    product[h % 4, :tall] = value
                for a in range(ANGLES):
                    moved = a * h // ANGLES
                    piece = product[h % 4, moved : moved + depth_out] if moved else value[:depth_out]
                    totals[a] = piece if totals[a] is None else totals[a] + piece
            for a in range(ANGLES):
                if g:
                    totals[a] = totals[a] + image[chunk, a, x]
                image[chunk, a, x] = totals[a]

    def core_copy(chunk):
        return pltpu.make_async_remote_copy(
            src_ref=image.at[chunk, pl.ds(angles_out * other, angles_out)],
            dst_ref=from_core.at[chunk],
            send_sem=core_send.at[chunk],
            recv_sem=core_recv.at[chunk],
            device_id={"shot": other},
            device_id_type=MESH,
        )

    def out_copy(j):
        return pltpu.make_async_remote_copy(
            src_ref=summed.at[j],
            dst_ref=from_pair.at[j],
            send_sem=out_send.at[j],
            recv_sem=out_recv.at[j],
            device_id={"gx": pair},
            device_id_type=MESH,
        )

    def pass_on(j):
        chunk = 2 * (1 - y) + j
        core_copy(chunk).wait_recv()

        @pl.loop(0, block)
        def _(x):
            for a in range(angles_out):
                summed[j, a, x] = image[chunk, angles_out * core + a, x] + from_core[chunk, a, x]

        out_copy(j).start()

    def finish(j):
        chunk = 2 * y + j
        core_copy(chunk).wait_recv()
        out_copy(j).wait_recv()

        @pl.loop(0, block)
        def _(x):
            for a in range(angles_out):
                value = image[chunk, angles_out * core + a, x] + from_core[chunk, a, x]
                out[a, j * block + x] = (value + from_pair[j, a, x]) * scale

    loads[0].wait()
    loads[1].wait()
    send_halo(0)
    for load in loads[2:]:
        load.wait()
    wave_step(0)
    send_halo(1)
    wave_step(1)
    send_halo(2)
    own_out(0)
    wave_step(2)
    send_halo(3)
    relay(0)
    wave_step(3)
    own_out(1)
    wait_window(0)

    @pl.loop(0, 4)
    def _(chunk):
        image_chunk(0, chunk)

    relay(1)
    wait_window(1)
    for j in range(2):
        image_chunk(1, 2 * (1 - y) + j)
        core_copy(2 * (1 - y) + j).start()
        if j:
            pass_on(0)
    for j in range(2):
        image_chunk(1, 2 * y + j)
        core_copy(2 * y + j).start()
        if j == 0:
            pass_on(1)
    for j in range(2):
        finish(j)

    for t in range(STEPS):
        @pl.when(me < n - 1)
        def _():
            halo(t, 0).wait_send()

        @pl.when(me > 0)
        def _():
            halo(t, 1).wait_send()

    for g in range(IMAGES):
        for part in range(2):
            pair_copy(g, part).wait_send()
        for k in range(3):
            @pl.when(has_above)
            def _():
                up_copy(g, k).wait_send()

            @pl.when(has_below)
            def _():
                down_copy(g, k).wait_send()

    for chunk in range(4):
        core_copy(chunk).wait_send()
    for j in range(2):
        out_copy(j).wait_send()


def solution(mesh):
    n = mesh.shape["gx"]
    cores = mesh.shape["shot"]

    def local(src_now, src_prev, rec_now, rec_prev, courant_sq, wavelet, traces, positions):
        shots, planes, depth, width = src_now.shape
        depth_out = depth // 2
        reach = depth_out + (ANGLES - 1) * HALF // ANGLES
        rows = min(depth, -(-(reach + STEPS - 1) // 8) * 8)
        block = planes // 2
        assert n % 2 == 0 and cores == 2 and shots == 2 and 3 * block == HALF
        angles_out = ANGLES // cores
        scale = 1.0 / math.sqrt(LAGS * shots * cores * IMAGES)
        vmem = pl.BlockSpec(memory_space=pltpu.VMEM)
        smem = pl.BlockSpec(memory_space=pltpu.SMEM)
        hbm = pl.BlockSpec(memory_space=pl.ANY)
        f32 = jnp.float32
        dma = pltpu.SemaphoreType.DMA
        return pl.pallas_call(
            functools.partial(kernel, n, scale, rows),
            out_shape=jax.ShapeDtypeStruct((angles_out, planes, depth_out, width), f32),
            in_specs=[smem] * 3 + [hbm] * 5,
            out_specs=vmem,
            scratch_shapes=[
                pltpu.VMEM((STEPS + 2, 2, shots, planes + 2, depth, width), f32),
                pltpu.VMEM((planes, depth, width), f32),
                pltpu.VMEM((IMAGES, 2, 2 * planes + 2 * HALF, rows, width), f32),
                pltpu.VMEM((4, ANGLES, block, depth_out, width), f32),
                pltpu.VMEM((4, angles_out, block, depth_out, width), f32),
                pltpu.VMEM((2, angles_out, block, depth_out, width), f32),
                pltpu.VMEM((2, angles_out, block, depth_out, width), f32),
                pltpu.VMEM((4, rows, width), f32),
                dma((5,)),
                dma((STEPS, 2)),
                dma((STEPS, 2)),
                dma((IMAGES, 2)),
                dma((IMAGES, 2)),
                dma((IMAGES, 3)),
                dma((IMAGES, 3)),
                dma((IMAGES, 3)),
                dma((IMAGES, 3)),
                dma((4,)),
                dma((4,)),
                dma((2,)),
                dma((2,)),
            ],
            compiler_params=pltpu.CompilerParams(
                collective_id=0, has_side_effects=True, vmem_limit_bytes=60 * 1024 * 1024
            ),
        )(positions, wavelet, traces, src_now, src_prev, rec_now, rec_prev, courant_sq)

    placed = (
        P(("groups", "shot"), "gx", None, None),
        P(("groups", "shot"), "gx", None, None),
        P(("groups", "shot"), "gx", None, None),
        P(("groups", "shot"), "gx", None, None),
        P(("groups", "gx"), None, None),
        P(("groups", "shot"), None),
        P(("groups", "shot"), None, "gx"),
        P(("groups", "shot"), None),
    )
    return jax.shard_map(
        local,
        mesh=mesh,
        in_specs=placed,
        out_specs=P(("groups", "shot"), "gx", None, None),
        check_vma=False,
    )
```

```python
import functools
import math

import jax
import jax.numpy as jnp
from jax import lax
from jax.experimental import pallas as pl
from jax.experimental.pallas import tpu as pltpu
from jax.sharding import PartitionSpec as P

STEPS = 4
IMAGES = 2
LAGS = 49
ANGLES = 8
HALF = (LAGS - 1) // 2
MESH = pl.DeviceIdType.MESH


def kernel(
    n,
    scale,
    rows,
    sent,
    positions,
    wavelet,
    traces,
    src_now,
    src_prev,
    rec_now,
    rec_prev,
    courant_hbm,
    out,
    level,
    courant,
    window,
    outgoing,
    image,
    from_core,
    summed,
    from_pair,
    product,
    load_sem,
    halo_send,
    halo_recv,
    pair_send,
    pair_recv,
    up_send,
    up_recv,
    down_send,
    down_recv,
    core_send,
    core_recv,
    out_send,
    out_recv,
):
    planes, depth, width = courant.shape
    block = planes // 2
    shots = src_now.shape[0]
    depth_out = out.shape[2]
    packs = from_core.shape[1]
    lanes = width // 2
    me = lax.axis_index("gx")
    core = lax.axis_index("shot")
    y = lax.rem(me, 2)
    pair = me + 1 - 2 * y
    other = 1 - core
    has_below = me >= 2
    has_above = me < n - 2

    loads = []
    for i, (ref, k, f) in enumerate(
        ((src_now, 1, 0), (rec_now, 1, 1), (src_prev, 0, 0), (rec_prev, 0, 1))
    ):
        loads.append(
            pltpu.make_async_copy(ref, level.at[k, f, :, pl.ds(1, planes)], load_sem.at[i])
        )
    loads.append(pltpu.make_async_copy(courant_hbm, courant, load_sem.at[4]))
    for load in loads:
        load.start()

    barrier = pltpu.get_barrier_semaphore()
    for step in (-2, -1, 1, 2):
        there = me + step

        @pl.when((there >= 0) & (there < n))
        def _():
            pl.semaphore_signal(barrier, inc=1, device_id={"gx": there}, device_id_type=MESH)

    pl.semaphore_signal(barrier, inc=1, device_id={"shot": other}, device_id_type=MESH)

    edge = jnp.zeros((rows, width), jnp.float32)
    full = jnp.zeros((depth, width), jnp.float32)

    @pl.when(me == 0)
    def _():
        for k in range(1, STEPS + 1):
            for f in range(2):
                for s in range(shots):
                    level[k, f, s, 0] = full

    @pl.when(me == n - 1)
    def _():
        for k in range(1, STEPS + 1):
            for f in range(2):
                for s in range(shots):
                    level[k, f, s, planes + 1] = full

    @pl.when(jnp.logical_not(has_below))
    def _():
        @pl.loop(0, HALF)
        def _(q):
            for g in range(IMAGES):
                for f in range(2):
                    window[g, f, q] = edge

    @pl.when(jnp.logical_not(has_above))
    def _():
        @pl.loop(0, HALF)
        def _(q):
            for g in range(IMAGES):
                for f in range(2):
                    window[g, f, HALF + 2 * planes + q] = edge

    peers = jnp.minimum(me, 2) + jnp.minimum(n - 1 - me, 2) + 1
    pl.semaphore_wait(barrier, peers)

    def halo(t, side):
        height = min(depth, rows + 1) if t == 0 else rows
        kept = pl.ds(0, height)
        source, target = (planes, 0) if side == 0 else (1, planes + 1)
        return pltpu.make_async_remote_copy(
            src_ref=level.at[1 + t, :, :, source, kept],
            dst_ref=level.at[1 + t, :, :, target, kept],
            send_sem=halo_send.at[t, side],
            recv_sem=halo_recv.at[t, side],
            device_id={"gx": me + 1 if side == 0 else me - 1},
            device_id_type=MESH,
        )

    def send_halo(t):
        @pl.when(me < n - 1)
        def _():
            halo(t, 0).start()

        @pl.when(me > 0)
        def _():
            halo(t, 1).start()

    def wait_halo(t):
        @pl.when(me > 0)
        def _():
            halo(t, 0).wait_recv()

        @pl.when(me < n - 1)
        def _():
            halo(t, 1).wait_recv()

    z_row = lax.broadcasted_iota(jnp.int32, (rows, width), 0)
    y_lane = lax.broadcasted_iota(jnp.int32, (rows, width), 1)
    first = me * planes

    def plane_step(t, x):
        speed = courant[x - 1, :rows]
        tall = depth if t == 0 else rows
        for s in range(shots):
            for f in range(2):
                now_tall = level[1 + t, f, s, x, :tall]
                now = now_tall[:rows]
                low = level[1 + t, f, s, x - 1, :rows]
                high = level[1 + t, f, s, x + 1, :rows]
                zeros = jnp.zeros((1, width), jnp.float32)
                deeper = jnp.concatenate([now_tall[1:], zeros], axis=0)[:rows]
                shallower = jnp.concatenate([zeros, now[: rows - 1]], axis=0)
                left = jnp.where(y_lane == 0, 0.0, pltpu.roll(now, 1, 1))
                right = jnp.where(y_lane == width - 1, 0.0, pltpu.roll(now, width - 1, 1))
                beside = low + high + deeper + shallower + left + right
                nxt = 2.0 * now - level[t, f, s, x, :rows] + speed * (beside - 6.0 * now)
                if f == 0:
                    amount = jnp.where(first + x - 1 == positions[s, 0], wavelet[s, t], 0.0)
                    hit = (z_row == positions[s, 2]) & (y_lane == positions[s, 1])
                else:
                    amount = traces[s, STEPS - 1 - t, x - 1]
                    hit = (z_row == 0) & (y_lane == positions[s, 3])
                level[2 + t, f, s, x, :rows] = nxt + jnp.where(hit, amount, 0.0)

    def wave_step(t):
        @pl.loop(2, planes)
        def _(x):
            plane_step(t, x)

        wait_halo(t)
        for half in range(2):
            @pl.loop(0, 1)
            def _(_i, half=half):
                plane_step(t, 1 + half * (planes - 1))

    def pair_copy(g, part):
        at = block * (1 - y) if part == 0 else block * y
        return pltpu.make_async_remote_copy(
            src_ref=outgoing.at[g, :, pl.ds(at, block), pl.ds(0, sent)],
            dst_ref=window.at[g, :, pl.ds(HALF + planes * y + at, block), pl.ds(0, sent)],
            send_sem=pair_send.at[g, part],
            recv_sem=pair_recv.at[g, part],
            device_id={"gx": pair},
            device_id_type=MESH,
        )

    def up_copy(g, k):
        return pltpu.make_async_remote_copy(
            src_ref=window.at[g, :, pl.ds(HALF + block * (k + 1), block), pl.ds(0, sent)],
            dst_ref=window.at[g, :, pl.ds(block * k, block), pl.ds(0, sent)],
            send_sem=up_send.at[g, k],
            recv_sem=up_recv.at[g, k],
            device_id={"gx": me + 2},
            device_id_type=MESH,
        )

    def down_copy(g, k):
        return pltpu.make_async_remote_copy(
            src_ref=window.at[g, :, pl.ds(HALF + block * k, block), pl.ds(0, sent)],
            dst_ref=window.at[g, :, pl.ds(HALF + 2 * planes + block * k, block), pl.ds(0, sent)],
            send_sem=down_send.at[g, k],
            recv_sem=down_recv.at[g, k],
            device_id={"gx": me - 2},
            device_id_type=MESH,
        )

    def send_inner(g, owner):
        @pl.when(has_above)
        def _():
            up_copy(g, owner).start()

        @pl.when(has_below)
        def _():
            down_copy(g, 1 + owner).start()

    def send_outer(g, owner):
        @pl.when(has_above & (owner == 1))
        def _():
            up_copy(g, 2).start()

        @pl.when(has_below & (owner == 0))
        def _():
            down_copy(g, 0).start()

    first_half = y_lane < lanes

    def own_out(g):
        @pl.loop(0, planes)
        def _(x):
            for f in range(2):
                one = level[2 * g + 3, f, 0, 1 + x, :rows]
                two = level[2 * g + 3, f, 1, 1 + x, :rows]
                halves = (
                    jnp.where(first_half, one, pltpu.roll(two, lanes, 1)),
                    jnp.where(first_half, pltpu.roll(one, lanes, 1), two),
                )
                window[g, f, HALF + planes * y + x] = jnp.where(y == 0, halves[0], halves[1])
                outgoing[g, f, x] = jnp.where(y == 0, halves[1], halves[0])

        pair_copy(g, 0).start()
        pair_copy(g, 1).start()
        send_inner(g, y)
        send_outer(g, y)

    def relay(g):
        pair_copy(g, 0).wait_recv()
        send_inner(g, 1 - y)
        pair_copy(g, 1).wait_recv()
        send_outer(g, 1 - y)

    def wait_window(g):
        for k in range(3):
            @pl.when(has_below)
            def _():
                up_copy(g, k).wait_recv()

            @pl.when(has_above)
            def _():
                down_copy(g, k).wait_recv()

    def image_chunk(g, chunk):
        @pl.loop(0, block)
        def _(x):
            at = HALF + chunk * block + x
            totals = [None] * ANGLES
            for h in range(HALF + 1):
                reach = depth_out + (ANGLES - 1) * h // ANGLES
                tall = min(rows, -(-reach // 8) * 8)
                value = window[g, 0, at - h, :tall] * window[g, 1, at + h, :tall]
                if h:
                    value = value + window[g, 0, at + h, :tall] * window[g, 1, at - h, :tall]
                if h > 1:
                    product[h % 4, :tall] = value
                for a in range(ANGLES):
                    moved = a * h // ANGLES
                    piece = product[h % 4, moved : moved + depth_out] if moved else value[:depth_out]
                    totals[a] = piece if totals[a] is None else totals[a] + piece
            for i in range(ANGLES // 2):
                even, odd = totals[2 * i], totals[2 * i + 1]
                low = first_half[:depth_out]
                folded = jnp.where(low, even, odd)
                folded = folded + pltpu.roll(jnp.where(low, odd, even), lanes, 1)
                if g:
                    folded = folded + image[chunk, i, x]
                image[chunk, i, x] = folded

    def core_copy(chunk):
        return pltpu.make_async_remote_copy(
            src_ref=image.at[chunk, pl.ds(packs * other, packs)],
            dst_ref=from_core.at[chunk],
            send_sem=core_send.at[chunk],
            recv_sem=core_recv.at[chunk],
            device_id={"shot": other},
            device_id_type=MESH,
        )

    def out_copy(j):
        return pltpu.make_async_remote_copy(
            src_ref=summed.at[j],
            dst_ref=from_pair.at[j],
            send_sem=out_send.at[j],
            recv_sem=out_recv.at[j],
            device_id={"gx": pair},
            device_id_type=MESH,
        )

    def pass_on(j):
        chunk = 2 * (1 - y) + j
        core_copy(chunk).wait_recv()

        @pl.loop(0, block)
        def _(x):
            for i in range(packs):
                summed[j, i, x] = image[chunk, packs * core + i, x] + from_core[chunk, i, x]

        out_copy(j).start()

    def finish(j):
        chunk = 2 * y + j
        core_copy(chunk).wait_recv()
        out_copy(j).wait_recv()

        @pl.loop(0, block)
        def _(x):
            low = first_half[:depth_out]
            for i in range(packs):
                mine = image[chunk, packs * core + i, x] + from_core[chunk, i, x]
                theirs = from_pair[j, i, x]
                left = jnp.where(y == 0, mine, theirs) * scale
                right = jnp.where(y == 0, theirs, mine) * scale
                out[2 * i, j * block + x] = jnp.where(low, left, pltpu.roll(right, lanes, 1))
                out[2 * i + 1, j * block + x] = jnp.where(low, pltpu.roll(left, lanes, 1), right)

    loads[0].wait()
    loads[1].wait()
    send_halo(0)
    for load in loads[2:]:
        load.wait()
    wave_step(0)
    send_halo(1)
    wave_step(1)
    send_halo(2)
    own_out(0)
    wave_step(2)
    send_halo(3)
    relay(0)
    wave_step(3)
    own_out(1)
    wait_window(0)

    @pl.loop(0, 4)
    def _(chunk):
        image_chunk(0, chunk)

    relay(1)
    wait_window(1)
    for j in range(2):
        image_chunk(1, 2 * (1 - y) + j)
        core_copy(2 * (1 - y) + j).start()
        if j:
            pass_on(0)
    for j in range(2):
        image_chunk(1, 2 * y + j)
        core_copy(2 * y + j).start()
        if j == 0:
            pass_on(1)
    for j in range(2):
        finish(j)

    for t in range(STEPS):
        @pl.when(me < n - 1)
        def _():
            halo(t, 0).wait_send()

        @pl.when(me > 0)
        def _():
            halo(t, 1).wait_send()

    for g in range(IMAGES):
        for part in range(2):
            pair_copy(g, part).wait_send()
        for k in range(3):
            @pl.when(has_above)
            def _():
                up_copy(g, k).wait_send()

            @pl.when(has_below)
            def _():
                down_copy(g, k).wait_send()

    for chunk in range(4):
        core_copy(chunk).wait_send()
    for j in range(2):
        out_copy(j).wait_send()


def solution(mesh):
    n = mesh.shape["gx"]
    cores = mesh.shape["shot"]

    def local(src_now, src_prev, rec_now, rec_prev, courant_sq, wavelet, traces, positions):
        shots, planes, depth, width = src_now.shape
        depth_out = depth // 2
        reach = depth_out + (ANGLES - 1) * HALF // ANGLES
        rows = min(depth, -(-(reach + STEPS - 1) // 8) * 8)
        block = planes // 2
        assert n % 2 == 0 and cores == 2 and shots == 2 and 3 * block == HALF and width % 2 == 0
        angles_out = ANGLES // cores
        scale = 1.0 / math.sqrt(LAGS * shots * cores * IMAGES)
        vmem = pl.BlockSpec(memory_space=pltpu.VMEM)
        smem = pl.BlockSpec(memory_space=pltpu.SMEM)
        hbm = pl.BlockSpec(memory_space=pl.ANY)
        f32 = jnp.float32
        dma = pltpu.SemaphoreType.DMA
        return pl.pallas_call(
            functools.partial(kernel, n, scale, rows, reach),
            out_shape=jax.ShapeDtypeStruct((angles_out, planes, depth_out, width), f32),
            in_specs=[smem] * 3 + [hbm] * 5,
            out_specs=vmem,
            scratch_shapes=[
                pltpu.VMEM((STEPS + 2, 2, shots, planes + 2, depth, width), f32),
                pltpu.VMEM((planes, depth, width), f32),
                pltpu.VMEM((IMAGES, 2, 2 * planes + 2 * HALF, rows, width), f32),
                pltpu.VMEM((IMAGES, 2, planes, rows, width), f32),
                pltpu.VMEM((4, ANGLES // 2, block, depth_out, width), f32),
                pltpu.VMEM((4, angles_out // 2, block, depth_out, width), f32),
                pltpu.VMEM((2, angles_out // 2, block, depth_out, width), f32),
                pltpu.VMEM((2, angles_out // 2, block, depth_out, width), f32),
                pltpu.VMEM((4, rows, width), f32),
                dma((5,)),
                dma((STEPS, 2)),
                dma((STEPS, 2)),
                dma((IMAGES, 2)),
                dma((IMAGES, 2)),
                dma((IMAGES, 3)),
                dma((IMAGES, 3)),
                dma((IMAGES, 3)),
                dma((IMAGES, 3)),
                dma((4,)),
                dma((4,)),
                dma((2,)),
                dma((2,)),
            ],
            compiler_params=pltpu.CompilerParams(
                collective_id=0, has_side_effects=True, vmem_limit_bytes=60 * 1024 * 1024
            ),
        )(positions, wavelet, traces, src_now, src_prev, rec_now, rec_prev, courant_sq)

    placed = (
        P(("groups", "shot"), "gx", None, None),
        P(("groups", "shot"), "gx", None, None),
        P(("groups", "shot"), "gx", None, None),
        P(("groups", "shot"), "gx", None, None),
        P(("groups", "gx"), None, None),
        P(("groups", "shot"), None),
        P(("groups", "shot"), None, "gx"),
        P(("groups", "shot"), None),
    )
    return jax.shard_map(
        local,
        mesh=mesh,
        in_specs=placed,
        out_specs=P(("groups", "shot"), "gx", None, None),
        check_vma=False,
    )
```

```python
import functools
import math

import jax
import jax.numpy as jnp
from jax import lax
from jax.experimental import pallas as pl
from jax.experimental.pallas import tpu as pltpu
from jax.sharding import PartitionSpec as P

STEPS = 4
IMAGES = 2
LAGS = 49
ANGLES = 8
HALF = (LAGS - 1) // 2
MESH = pl.DeviceIdType.MESH


def kernel(
    n,
    scale,
    rows,
    sent,
    positions,
    wavelet,
    traces,
    src_now,
    src_prev,
    rec_now,
    rec_prev,
    courant_hbm,
    out,
    level,
    courant,
    window,
    outgoing,
    image,
    from_core,
    summed,
    from_pair,
    product,
    load_sem,
    halo_send,
    halo_recv,
    pair_send,
    pair_recv,
    up_send,
    up_recv,
    down_send,
    down_recv,
    core_send,
    core_recv,
    out_send,
    out_recv,
):
    planes, depth, width = courant.shape
    block = planes // 2
    shots = src_now.shape[0]
    depth_out = out.shape[2]
    packs = from_core.shape[1]
    lanes = width // 2
    me = lax.axis_index("gx")
    core = lax.axis_index("shot")
    y = lax.rem(me, 2)
    pair = me + 1 - 2 * y
    other = 1 - core
    has_below = me >= 2
    has_above = me < n - 2

    loads = []
    for i, (ref, k, f) in enumerate(
        ((src_now, 1, 0), (rec_now, 1, 1), (src_prev, 0, 0), (rec_prev, 0, 1))
    ):
        loads.append(
            pltpu.make_async_copy(ref, level.at[k, f, :, pl.ds(1, planes)], load_sem.at[i])
        )
    loads.append(pltpu.make_async_copy(courant_hbm, courant, load_sem.at[4]))
    for load in loads:
        load.start()

    barrier = pltpu.get_barrier_semaphore()
    for step in (-2, -1, 1, 2):
        there = me + step

        @pl.when((there >= 0) & (there < n))
        def _():
            pl.semaphore_signal(barrier, inc=1, device_id={"gx": there}, device_id_type=MESH)

    pl.semaphore_signal(barrier, inc=1, device_id={"shot": other}, device_id_type=MESH)

    edge = jnp.zeros((rows, width), jnp.float32)
    full = jnp.zeros((depth, width), jnp.float32)

    @pl.when(me == 0)
    def _():
        for k in range(1, STEPS + 1):
            for f in range(2):
                for s in range(shots):
                    level[k, f, s, 0] = full

    @pl.when(me == n - 1)
    def _():
        for k in range(1, STEPS + 1):
            for f in range(2):
                for s in range(shots):
                    level[k, f, s, planes + 1] = full

    @pl.when(jnp.logical_not(has_below))
    def _():
        @pl.loop(0, HALF)
        def _(q):
            for g in range(IMAGES):
                for f in range(2):
                    window[g, f, q] = edge

    @pl.when(jnp.logical_not(has_above))
    def _():
        @pl.loop(0, HALF)
        def _(q):
            for g in range(IMAGES):
                for f in range(2):
                    window[g, f, HALF + 2 * planes + q] = edge

    peers = jnp.minimum(me, 2) + jnp.minimum(n - 1 - me, 2) + 1
    pl.semaphore_wait(barrier, peers)

    def halo(t, side):
        height = min(depth, rows + 1) if t == 0 else rows
        kept = pl.ds(0, height)
        source, target = (planes, 0) if side == 0 else (1, planes + 1)
        return pltpu.make_async_remote_copy(
            src_ref=level.at[1 + t, :, :, source, kept],
            dst_ref=level.at[1 + t, :, :, target, kept],
            send_sem=halo_send.at[t, side],
            recv_sem=halo_recv.at[t, side],
            device_id={"gx": me + 1 if side == 0 else me - 1},
            device_id_type=MESH,
        )

    def send_halo(t):
        @pl.when(me < n - 1)
        def _():
            halo(t, 0).start()

        @pl.when(me > 0)
        def _():
            halo(t, 1).start()

    def wait_halo(t):
        @pl.when(me > 0)
        def _():
            halo(t, 0).wait_recv()

        @pl.when(me < n - 1)
        def _():
            halo(t, 1).wait_recv()

    z_row = lax.broadcasted_iota(jnp.int32, (rows, width), 0)
    y_lane = lax.broadcasted_iota(jnp.int32, (rows, width), 1)
    first = me * planes

    def plane_step(t, x):
        speed = courant[x - 1, :rows]
        tall = depth if t == 0 else rows
        for s in range(shots):
            for f in range(2):
                now_tall = level[1 + t, f, s, x, :tall]
                now = now_tall[:rows]
                low = level[1 + t, f, s, x - 1, :rows]
                high = level[1 + t, f, s, x + 1, :rows]
                zeros = jnp.zeros((1, width), jnp.float32)
                deeper = jnp.concatenate([now_tall[1:], zeros], axis=0)[:rows]
                shallower = jnp.concatenate([zeros, now[: rows - 1]], axis=0)
                left = jnp.where(y_lane == 0, 0.0, pltpu.roll(now, 1, 1))
                right = jnp.where(y_lane == width - 1, 0.0, pltpu.roll(now, width - 1, 1))
                beside = low + high + deeper + shallower + left + right
                nxt = 2.0 * now - level[t, f, s, x, :rows] + speed * (beside - 6.0 * now)
                if f == 0:
                    amount = jnp.where(first + x - 1 == positions[s, 0], wavelet[s, t], 0.0)
                    hit = (z_row == positions[s, 2]) & (y_lane == positions[s, 1])
                else:
                    amount = traces[s, STEPS - 1 - t, x - 1]
                    hit = (z_row == 0) & (y_lane == positions[s, 3])
                level[2 + t, f, s, x, :rows] = nxt + jnp.where(hit, amount, 0.0)

    def wave_step(t):
        @pl.loop(2, planes)
        def _(x):
            plane_step(t, x)

        wait_halo(t)
        for half in range(2):
            @pl.loop(0, 1)
            def _(_i, half=half):
                plane_step(t, 1 + half * (planes - 1))

    def pair_copy(g, part):
        at = block * (1 - y) if part == 0 else block * y
        return pltpu.make_async_remote_copy(
            src_ref=outgoing.at[g, :, pl.ds(at, block), pl.ds(0, sent)],
            dst_ref=window.at[g, :, pl.ds(HALF + planes * y + at, block), pl.ds(0, sent)],
            send_sem=pair_send.at[g, part],
            recv_sem=pair_recv.at[g, part],
            device_id={"gx": pair},
            device_id_type=MESH,
        )

    def up_copy(g, k):
        return pltpu.make_async_remote_copy(
            src_ref=window.at[g, :, pl.ds(HALF + block * (k + 1), block), pl.ds(0, sent)],
            dst_ref=window.at[g, :, pl.ds(block * k, block), pl.ds(0, sent)],
            send_sem=up_send.at[g, k],
            recv_sem=up_recv.at[g, k],
            device_id={"gx": me + 2},
            device_id_type=MESH,
        )

    def down_copy(g, k):
        return pltpu.make_async_remote_copy(
            src_ref=window.at[g, :, pl.ds(HALF + block * k, block), pl.ds(0, sent)],
            dst_ref=window.at[g, :, pl.ds(HALF + 2 * planes + block * k, block), pl.ds(0, sent)],
            send_sem=down_send.at[g, k],
            recv_sem=down_recv.at[g, k],
            device_id={"gx": me - 2},
            device_id_type=MESH,
        )

    def send_inner(g, owner):
        @pl.when(has_above)
        def _():
            up_copy(g, owner).start()

        @pl.when(has_below)
        def _():
            down_copy(g, 1 + owner).start()

    def send_outer(g, owner):
        @pl.when(has_above & (owner == 1))
        def _():
            up_copy(g, 2).start()

        @pl.when(has_below & (owner == 0))
        def _():
            down_copy(g, 0).start()

    first_half = y_lane < lanes

    def order(g):
        return (0, 1) if g == 0 else (1, 0)

    def own_out(g):
        for part in order(g):
            at = block * (1 - y) if part == 0 else block * y

            @pl.loop(0, block)
            def _(i, at=at):
                x = at + i
                for f in range(2):
                    one = level[2 * g + 3, f, 0, 1 + x, :rows]
                    two = level[2 * g + 3, f, 1, 1 + x, :rows]
                    halves = (
                        jnp.where(first_half, one, pltpu.roll(two, lanes, 1)),
                        jnp.where(first_half, pltpu.roll(one, lanes, 1), two),
                    )
                    window[g, f, HALF + planes * y + x] = jnp.where(y == 0, halves[0], halves[1])
                    outgoing[g, f, x] = jnp.where(y == 0, halves[1], halves[0])

            pair_copy(g, part).start()
            (send_outer if part else send_inner)(g, y)

    def relay(g):
        for part in order(g):
            pair_copy(g, part).wait_recv()
            (send_outer if part else send_inner)(g, 1 - y)

    def wait_block(g, late, distance):
        below = (y == 0) if late else (y == 1)

        @pl.when(below & has_below)
        def _():
            up_copy(g, 2 - distance).wait_recv()

        @pl.when(jnp.logical_not(below) & has_above)
        def _():
            down_copy(g, distance).wait_recv()

    def wait_window(g):
        for k in range(3):
            @pl.when(has_below)
            def _():
                up_copy(g, k).wait_recv()

            @pl.when(has_above)
            def _():
                down_copy(g, k).wait_recv()

    def image_chunk(g, chunk, lags):
        @pl.loop(0, block)
        def _(x):
            at = HALF + chunk * block + x
            totals = [None] * ANGLES
            for h in lags:
                reach = depth_out + (ANGLES - 1) * h // ANGLES
                tall = min(rows, -(-reach // 8) * 8)
                value = window[g, 0, at - h, :tall] * window[g, 1, at + h, :tall]
                if h:
                    value = value + window[g, 0, at + h, :tall] * window[g, 1, at - h, :tall]
                if h > 1:
                    product[h % 4, :tall] = value
                for a in range(ANGLES):
                    moved = a * h // ANGLES
                    piece = product[h % 4, moved : moved + depth_out] if moved else value[:depth_out]
                    totals[a] = piece if totals[a] is None else totals[a] + piece
            for i in range(ANGLES // 2):
                even, odd = totals[2 * i], totals[2 * i + 1]
                low = first_half[:depth_out]
                folded = jnp.where(low, even, odd)
                folded = folded + pltpu.roll(jnp.where(low, odd, even), lanes, 1)
                if g:
                    folded = folded + image[chunk, i, x]
                image[chunk, i, x] = folded

    def core_copy(chunk):
        return pltpu.make_async_remote_copy(
            src_ref=image.at[chunk, pl.ds(packs * other, packs)],
            dst_ref=from_core.at[chunk],
            send_sem=core_send.at[chunk],
            recv_sem=core_recv.at[chunk],
            device_id={"shot": other},
            device_id_type=MESH,
        )

    def out_copy(j):
        return pltpu.make_async_remote_copy(
            src_ref=summed.at[j],
            dst_ref=from_pair.at[j],
            send_sem=out_send.at[j],
            recv_sem=out_recv.at[j],
            device_id={"gx": pair},
            device_id_type=MESH,
        )

    def pass_on(chunk):
        j = chunk - 2 * (1 - y)
        core_copy(chunk).wait_recv()

        @pl.loop(0, block)
        def _(x):
            for i in range(packs):
                summed[j, i, x] = image[chunk, packs * core + i, x] + from_core[chunk, i, x]

        out_copy(j).start()

    def finish(j):
        chunk = 2 * y + j
        core_copy(chunk).wait_recv()
        out_copy(j).wait_recv()

        @pl.loop(0, block)
        def _(x):
            low = first_half[:depth_out]
            for i in range(packs):
                mine = image[chunk, packs * core + i, x] + from_core[chunk, i, x]
                theirs = from_pair[j, i, x]
                left = jnp.where(y == 0, mine, theirs) * scale
                right = jnp.where(y == 0, theirs, mine) * scale
                out[2 * i, j * block + x] = jnp.where(low, left, pltpu.roll(right, lanes, 1))
                out[2 * i + 1, j * block + x] = jnp.where(low, pltpu.roll(left, lanes, 1), right)

    loads[0].wait()
    loads[1].wait()
    send_halo(0)
    for load in loads[2:]:
        load.wait()
    wave_step(0)
    send_halo(1)
    wave_step(1)
    send_halo(2)
    own_out(0)
    wave_step(2)
    send_halo(3)
    relay(0)
    wave_step(3)
    own_out(1)
    wait_window(0)
    near, far = range(block + 1), range(2 * block + 1, HALF + 1)

    @pl.loop(0, 4)
    def _(chunk):
        image_chunk(0, chunk, range(HALF + 1))

    relay(1)
    chunks = [c + y * (3 - 2 * c) for c in range(4)]
    wait_block(1, False, 0)
    wait_block(1, False, 1)

    @pl.loop(2, 4)
    def _(c):
        image_chunk(1, c + y * (3 - 2 * c), range(2 * block + 1))

    wait_block(1, True, 0)
    image_chunk(1, chunks[2], far)
    core_copy(chunks[2]).start()
    image_chunk(1, chunks[1], range(2 * block + 1))
    pass_on(chunks[2])
    image_chunk(1, chunks[0], near)
    wait_block(1, False, 2)
    image_chunk(1, chunks[3], far)
    core_copy(chunks[3]).start()
    wait_block(1, True, 1)
    wait_block(1, True, 2)
    image_chunk(1, chunks[1], far)
    core_copy(chunks[1]).start()
    pass_on(chunks[3])
    image_chunk(1, chunks[0], range(block + 1, HALF + 1))
    core_copy(chunks[0]).start()
    finish(1 - y)
    finish(y)

    for t in range(STEPS):
        @pl.when(me < n - 1)
        def _():
            halo(t, 0).wait_send()

        @pl.when(me > 0)
        def _():
            halo(t, 1).wait_send()

    for g in range(IMAGES):
        for part in range(2):
            pair_copy(g, part).wait_send()
        for k in range(3):
            @pl.when(has_above)
            def _():
                up_copy(g, k).wait_send()

            @pl.when(has_below)
            def _():
                down_copy(g, k).wait_send()

    for chunk in range(4):
        core_copy(chunk).wait_send()
    for j in range(2):
        out_copy(j).wait_send()


def solution(mesh):
    n = mesh.shape["gx"]
    cores = mesh.shape["shot"]

    def local(src_now, src_prev, rec_now, rec_prev, courant_sq, wavelet, traces, positions):
        shots, planes, depth, width = src_now.shape
        depth_out = depth // 2
        reach = depth_out + (ANGLES - 1) * HALF // ANGLES
        rows = min(depth, -(-(reach + STEPS - 1) // 8) * 8)
        block = planes // 2
        assert n % 2 == 0 and cores == 2 and shots == 2 and 3 * block == HALF and width % 2 == 0
        angles_out = ANGLES // cores
        scale = 1.0 / math.sqrt(LAGS * shots * cores * IMAGES)
        vmem = pl.BlockSpec(memory_space=pltpu.VMEM)
        smem = pl.BlockSpec(memory_space=pltpu.SMEM)
        hbm = pl.BlockSpec(memory_space=pl.ANY)
        f32 = jnp.float32
        dma = pltpu.SemaphoreType.DMA
        return pl.pallas_call(
            functools.partial(kernel, n, scale, rows, reach),
            out_shape=jax.ShapeDtypeStruct((angles_out, planes, depth_out, width), f32),
            in_specs=[smem] * 3 + [hbm] * 5,
            out_specs=vmem,
            scratch_shapes=[
                pltpu.VMEM((STEPS + 2, 2, shots, planes + 2, depth, width), f32),
                pltpu.VMEM((planes, depth, width), f32),
                pltpu.VMEM((IMAGES, 2, 2 * planes + 2 * HALF, rows, width), f32),
                pltpu.VMEM((IMAGES, 2, planes, rows, width), f32),
                pltpu.VMEM((4, ANGLES // 2, block, depth_out, width), f32),
                pltpu.VMEM((4, angles_out // 2, block, depth_out, width), f32),
                pltpu.VMEM((2, angles_out // 2, block, depth_out, width), f32),
                pltpu.VMEM((2, angles_out // 2, block, depth_out, width), f32),
                pltpu.VMEM((4, rows, width), f32),
                dma((5,)),
                dma((STEPS, 2)),
                dma((STEPS, 2)),
                dma((IMAGES, 2)),
                dma((IMAGES, 2)),
                dma((IMAGES, 3)),
                dma((IMAGES, 3)),
                dma((IMAGES, 3)),
                dma((IMAGES, 3)),
                dma((4,)),
                dma((4,)),
                dma((2,)),
                dma((2,)),
            ],
            compiler_params=pltpu.CompilerParams(
                collective_id=0, has_side_effects=True, vmem_limit_bytes=60 * 1024 * 1024
            ),
        )(positions, wavelet, traces, src_now, src_prev, rec_now, rec_prev, courant_sq)

    placed = (
        P(("groups", "shot"), "gx", None, None),
        P(("groups", "shot"), "gx", None, None),
        P(("groups", "shot"), "gx", None, None),
        P(("groups", "shot"), "gx", None, None),
        P(("groups", "gx"), None, None),
        P(("groups", "shot"), None),
        P(("groups", "shot"), None, "gx"),
        P(("groups", "shot"), None),
    )
    return jax.shard_map(
        local,
        mesh=mesh,
        in_specs=placed,
        out_specs=P(("groups", "shot"), "gx", None, None),
        check_vma=False,
    )
```

```python
import functools
import math

import jax
import jax.numpy as jnp
from jax import lax
from jax.experimental import pallas as pl
from jax.experimental.pallas import tpu as pltpu
from jax.sharding import PartitionSpec as P

STEPS = 4
IMAGES = 2
LAGS = 49
ANGLES = 8
HALF = (LAGS - 1) // 2
MESH = pl.DeviceIdType.MESH


def kernel(
    n,
    scale,
    rows,
    sent,
    positions,
    wavelet,
    traces,
    src_now,
    src_prev,
    rec_now,
    rec_prev,
    courant_hbm,
    out,
    level,
    courant,
    window,
    outgoing,
    image,
    from_core,
    summed,
    from_pair,
    product,
    load_sem,
    halo_send,
    halo_recv,
    pair_send,
    pair_recv,
    up_send,
    up_recv,
    down_send,
    down_recv,
    core_send,
    core_recv,
    out_send,
    out_recv,
):
    planes, depth, width = courant.shape
    block = planes // 2
    shots = src_now.shape[0]
    depth_out = out.shape[2]
    packs = from_core.shape[1]
    lanes = width // 2
    me = lax.axis_index("gx")
    core = lax.axis_index("shot")
    y = lax.rem(me, 2)
    pair = me + 1 - 2 * y
    other = 1 - core
    has_below = me >= 2
    has_above = me < n - 2

    loads = []
    for i, (ref, k, f) in enumerate(
        ((src_now, 1, 0), (rec_now, 1, 1), (src_prev, 0, 0), (rec_prev, 0, 1))
    ):
        loads.append(
            pltpu.make_async_copy(ref, level.at[k, f, :, pl.ds(1, planes)], load_sem.at[i])
        )
    loads.append(pltpu.make_async_copy(courant_hbm, courant, load_sem.at[4]))
    for load in loads:
        load.start()

    barrier = pltpu.get_barrier_semaphore()
    for step in (-2, -1, 1, 2):
        there = me + step

        @pl.when((there >= 0) & (there < n))
        def _():
            pl.semaphore_signal(barrier, inc=1, device_id={"gx": there}, device_id_type=MESH)

    pl.semaphore_signal(barrier, inc=1, device_id={"shot": other}, device_id_type=MESH)

    edge = jnp.zeros((rows, width), jnp.float32)
    full = jnp.zeros((depth, width), jnp.float32)

    @pl.when(me == 0)
    def _():
        for k in range(1, STEPS + 1):
            for f in range(2):
                for s in range(shots):
                    level[k, f, s, 0] = full

    @pl.when(me == n - 1)
    def _():
        for k in range(1, STEPS + 1):
            for f in range(2):
                for s in range(shots):
                    level[k, f, s, planes + 1] = full

    @pl.when(jnp.logical_not(has_below))
    def _():
        @pl.loop(0, HALF)
        def _(q):
            for g in range(IMAGES):
                for f in range(2):
                    window[g, f, q] = edge

    @pl.when(jnp.logical_not(has_above))
    def _():
        @pl.loop(0, HALF)
        def _(q):
            for g in range(IMAGES):
                for f in range(2):
                    window[g, f, HALF + 2 * planes + q] = edge

    peers = jnp.minimum(me, 2) + jnp.minimum(n - 1 - me, 2) + 1
    pl.semaphore_wait(barrier, peers)

    def halo(t, side):
        height = min(depth, rows + 1) if t == 0 else rows
        kept = pl.ds(0, height)
        source, target = (planes, 0) if side == 0 else (1, planes + 1)
        return pltpu.make_async_remote_copy(
            src_ref=level.at[1 + t, :, :, source, kept],
            dst_ref=level.at[1 + t, :, :, target, kept],
            send_sem=halo_send.at[t, side],
            recv_sem=halo_recv.at[t, side],
            device_id={"gx": me + 1 if side == 0 else me - 1},
            device_id_type=MESH,
        )

    def send_halo(t):
        @pl.when(me < n - 1)
        def _():
            halo(t, 0).start()

        @pl.when(me > 0)
        def _():
            halo(t, 1).start()

    def wait_halo(t):
        @pl.when(me > 0)
        def _():
            halo(t, 0).wait_recv()

        @pl.when(me < n - 1)
        def _():
            halo(t, 1).wait_recv()

    z_row = lax.broadcasted_iota(jnp.int32, (rows, width), 0)
    y_lane = lax.broadcasted_iota(jnp.int32, (rows, width), 1)
    first = me * planes

    def plane_step(t, x):
        speed = courant[x - 1, :rows]
        tall = depth if t == 0 else rows
        for s in range(shots):
            for f in range(2):
                now_tall = level[1 + t, f, s, x, :tall]
                now = now_tall[:rows]
                low = level[1 + t, f, s, x - 1, :rows]
                high = level[1 + t, f, s, x + 1, :rows]
                zeros = jnp.zeros((1, width), jnp.float32)
                deeper = jnp.concatenate([now_tall[1:], zeros], axis=0)[:rows]
                shallower = jnp.concatenate([zeros, now[: rows - 1]], axis=0)
                left = jnp.where(y_lane == 0, 0.0, pltpu.roll(now, 1, 1))
                right = jnp.where(y_lane == width - 1, 0.0, pltpu.roll(now, width - 1, 1))
                beside = low + high + deeper + shallower + left + right
                nxt = 2.0 * now - level[t, f, s, x, :rows] + speed * (beside - 6.0 * now)
                if f == 0:
                    amount = jnp.where(first + x - 1 == positions[s, 0], wavelet[s, t], 0.0)
                    hit = (z_row == positions[s, 2]) & (y_lane == positions[s, 1])
                else:
                    amount = traces[s, STEPS - 1 - t, x - 1]
                    hit = (z_row == 0) & (y_lane == positions[s, 3])
                level[2 + t, f, s, x, :rows] = nxt + jnp.where(hit, amount, 0.0)

    def wave_step(t):
        @pl.loop(2, planes)
        def _(x):
            plane_step(t, x)

        wait_halo(t)
        for half in range(2):
            @pl.loop(0, 1)
            def _(_i, half=half):
                plane_step(t, 1 + half * (planes - 1))

    def pair_copy(g, part):
        at = block * (1 - y) if part == 0 else block * y
        return pltpu.make_async_remote_copy(
            src_ref=outgoing.at[g, :, pl.ds(at, block), pl.ds(0, sent)],
            dst_ref=window.at[g, :, pl.ds(HALF + planes * y + at, block), pl.ds(0, sent)],
            send_sem=pair_send.at[g, part],
            recv_sem=pair_recv.at[g, part],
            device_id={"gx": pair},
            device_id_type=MESH,
        )

    def up_copy(g, k):
        return pltpu.make_async_remote_copy(
            src_ref=window.at[g, :, pl.ds(HALF + block * (k + 1), block), pl.ds(0, sent)],
            dst_ref=window.at[g, :, pl.ds(block * k, block), pl.ds(0, sent)],
            send_sem=up_send.at[g, k],
            recv_sem=up_recv.at[g, k],
            device_id={"gx": me + 2},
            device_id_type=MESH,
        )

    def down_copy(g, k):
        return pltpu.make_async_remote_copy(
            src_ref=window.at[g, :, pl.ds(HALF + block * k, block), pl.ds(0, sent)],
            dst_ref=window.at[g, :, pl.ds(HALF + 2 * planes + block * k, block), pl.ds(0, sent)],
            send_sem=down_send.at[g, k],
            recv_sem=down_recv.at[g, k],
            device_id={"gx": me - 2},
            device_id_type=MESH,
        )

    def send_inner(g, owner):
        @pl.when(has_above)
        def _():
            up_copy(g, owner).start()

        @pl.when(has_below)
        def _():
            down_copy(g, 1 + owner).start()

    def send_outer(g, owner):
        @pl.when(has_above & (owner == 1))
        def _():
            up_copy(g, 2).start()

        @pl.when(has_below & (owner == 0))
        def _():
            down_copy(g, 0).start()

    first_half = y_lane < lanes

    def order(g):
        return (0, 1) if g == 0 else (1, 0)

    def own_out(g):
        for part in order(g):
            at = block * (1 - y) if part == 0 else block * y

            @pl.loop(0, block)
            def _(i, at=at):
                x = at + i
                for f in range(2):
                    one = level[2 * g + 3, f, 0, 1 + x, :rows]
                    two = level[2 * g + 3, f, 1, 1 + x, :rows]
                    halves = (
                        jnp.where(first_half, one, pltpu.roll(two, lanes, 1)),
                        jnp.where(first_half, pltpu.roll(one, lanes, 1), two),
                    )
                    window[g, f, HALF + planes * y + x] = jnp.where(y == 0, halves[0], halves[1])
                    outgoing[g, f, x] = jnp.where(y == 0, halves[1], halves[0])

            pair_copy(g, part).start()
            (send_outer if part else send_inner)(g, y)

    def relay(g, parts):
        for part in parts:
            pair_copy(g, part).wait_recv()
            (send_outer if part else send_inner)(g, 1 - y)

    def wait_block(g, late, distance):
        below = (y == 0) if late else (y == 1)

        @pl.when(below & has_below)
        def _():
            up_copy(g, 2 - distance).wait_recv()

        @pl.when(jnp.logical_not(below) & has_above)
        def _():
            down_copy(g, distance).wait_recv()

    def wait_window(g):
        for k in range(3):
            @pl.when(has_below)
            def _():
                up_copy(g, k).wait_recv()

            @pl.when(has_above)
            def _():
                down_copy(g, k).wait_recv()

    def image_chunk(g, chunk, lags):
        @pl.loop(0, block)
        def _(x):
            at = HALF + chunk * block + x
            totals = [None] * ANGLES
            for h in lags:
                reach = depth_out + (ANGLES - 1) * h // ANGLES
                tall = min(rows, -(-reach // 8) * 8)
                value = window[g, 0, at - h, :tall] * window[g, 1, at + h, :tall]
                if h:
                    value = value + window[g, 0, at + h, :tall] * window[g, 1, at - h, :tall]
                if h > 1:
                    product[h % 4, :tall] = value
                for a in range(ANGLES):
                    moved = a * h // ANGLES
                    piece = product[h % 4, moved : moved + depth_out] if moved else value[:depth_out]
                    totals[a] = piece if totals[a] is None else totals[a] + piece
            for i in range(ANGLES // 2):
                even, odd = totals[2 * i], totals[2 * i + 1]
                low = first_half[:depth_out]
                folded = jnp.where(low, even, odd)
                folded = folded + pltpu.roll(jnp.where(low, odd, even), lanes, 1)
                if g:
                    folded = folded + image[chunk, i, x]
                image[chunk, i, x] = folded

    def core_copy(chunk):
        return pltpu.make_async_remote_copy(
            src_ref=image.at[chunk, pl.ds(packs * other, packs)],
            dst_ref=from_core.at[chunk],
            send_sem=core_send.at[chunk],
            recv_sem=core_recv.at[chunk],
            device_id={"shot": other},
            device_id_type=MESH,
        )

    def out_copy(j):
        return pltpu.make_async_remote_copy(
            src_ref=summed.at[j],
            dst_ref=from_pair.at[j],
            send_sem=out_send.at[j],
            recv_sem=out_recv.at[j],
            device_id={"gx": pair},
            device_id_type=MESH,
        )

    def pass_on(chunk):
        j = chunk - 2 * (1 - y)
        core_copy(chunk).wait_recv()

        @pl.loop(0, block)
        def _(x):
            for i in range(packs):
                summed[j, i, x] = image[chunk, packs * core + i, x] + from_core[chunk, i, x]

        out_copy(j).start()

    def finish(j):
        chunk = 2 * y + j
        core_copy(chunk).wait_recv()
        out_copy(j).wait_recv()

        @pl.loop(0, block)
        def _(x):
            low = first_half[:depth_out]
            for i in range(packs):
                mine = image[chunk, packs * core + i, x] + from_core[chunk, i, x]
                theirs = from_pair[j, i, x]
                left = jnp.where(y == 0, mine, theirs) * scale
                right = jnp.where(y == 0, theirs, mine) * scale
                out[2 * i, j * block + x] = jnp.where(low, left, pltpu.roll(right, lanes, 1))
                out[2 * i + 1, j * block + x] = jnp.where(low, pltpu.roll(left, lanes, 1), right)

    loads[0].wait()
    loads[1].wait()
    send_halo(0)
    for load in loads[2:]:
        load.wait()
    wave_step(0)
    send_halo(1)
    wave_step(1)
    send_halo(2)
    own_out(0)
    wave_step(2)
    send_halo(3)
    relay(0, order(0))
    wave_step(3)
    own_out(1)
    wait_window(0)
    near, far = range(block + 1), range(2 * block + 1, HALF + 1)

    @pl.loop(0, 2)
    def _(chunk):
        image_chunk(0, chunk, range(HALF + 1))

    relay(1, (1,))

    @pl.loop(2, 4)
    def _(chunk):
        image_chunk(0, chunk, range(HALF + 1))

    relay(1, (0,))
    chunks = [c + y * (3 - 2 * c) for c in range(4)]
    wait_block(1, False, 0)
    wait_block(1, False, 1)

    @pl.loop(2, 4)
    def _(c):
        image_chunk(1, c + y * (3 - 2 * c), range(2 * block + 1))

    wait_block(1, True, 0)
    image_chunk(1, chunks[2], far)
    core_copy(chunks[2]).start()
    image_chunk(1, chunks[1], range(2 * block + 1))
    pass_on(chunks[2])
    image_chunk(1, chunks[0], near)
    wait_block(1, False, 2)
    image_chunk(1, chunks[3], far)
    core_copy(chunks[3]).start()
    wait_block(1, True, 1)
    wait_block(1, True, 2)
    image_chunk(1, chunks[1], far)
    core_copy(chunks[1]).start()
    pass_on(chunks[3])
    image_chunk(1, chunks[0], range(block + 1, HALF + 1))
    core_copy(chunks[0]).start()
    finish(1 - y)
    finish(y)

    for t in range(STEPS):
        @pl.when(me < n - 1)
        def _():
            halo(t, 0).wait_send()

        @pl.when(me > 0)
        def _():
            halo(t, 1).wait_send()

    for g in range(IMAGES):
        for part in range(2):
            pair_copy(g, part).wait_send()
        for k in range(3):
            @pl.when(has_above)
            def _():
                up_copy(g, k).wait_send()

            @pl.when(has_below)
            def _():
                down_copy(g, k).wait_send()

    for chunk in range(4):
        core_copy(chunk).wait_send()
    for j in range(2):
        out_copy(j).wait_send()


def solution(mesh):
    n = mesh.shape["gx"]
    cores = mesh.shape["shot"]

    def local(src_now, src_prev, rec_now, rec_prev, courant_sq, wavelet, traces, positions):
        shots, planes, depth, width = src_now.shape
        depth_out = depth // 2
        reach = depth_out + (ANGLES - 1) * HALF // ANGLES
        rows = min(depth, -(-(reach + STEPS - 1) // 8) * 8)
        block = planes // 2
        assert n % 2 == 0 and cores == 2 and shots == 2 and 3 * block == HALF and width % 2 == 0
        angles_out = ANGLES // cores
        scale = 1.0 / math.sqrt(LAGS * shots * cores * IMAGES)
        vmem = pl.BlockSpec(memory_space=pltpu.VMEM)
        smem = pl.BlockSpec(memory_space=pltpu.SMEM)
        hbm = pl.BlockSpec(memory_space=pl.ANY)
        f32 = jnp.float32
        dma = pltpu.SemaphoreType.DMA
        return pl.pallas_call(
            functools.partial(kernel, n, scale, rows, reach),
            out_shape=jax.ShapeDtypeStruct((angles_out, planes, depth_out, width), f32),
            in_specs=[smem] * 3 + [hbm] * 5,
            out_specs=vmem,
            scratch_shapes=[
                pltpu.VMEM((STEPS + 2, 2, shots, planes + 2, depth, width), f32),
                pltpu.VMEM((planes, depth, width), f32),
                pltpu.VMEM((IMAGES, 2, 2 * planes + 2 * HALF, rows, width), f32),
                pltpu.VMEM((IMAGES, 2, planes, rows, width), f32),
                pltpu.VMEM((4, ANGLES // 2, block, depth_out, width), f32),
                pltpu.VMEM((4, angles_out // 2, block, depth_out, width), f32),
                pltpu.VMEM((2, angles_out // 2, block, depth_out, width), f32),
                pltpu.VMEM((2, angles_out // 2, block, depth_out, width), f32),
                pltpu.VMEM((4, rows, width), f32),
                dma((5,)),
                dma((STEPS, 2)),
                dma((STEPS, 2)),
                dma((IMAGES, 2)),
                dma((IMAGES, 2)),
                dma((IMAGES, 3)),
                dma((IMAGES, 3)),
                dma((IMAGES, 3)),
                dma((IMAGES, 3)),
                dma((4,)),
                dma((4,)),
                dma((2,)),
                dma((2,)),
            ],
            compiler_params=pltpu.CompilerParams(
                collective_id=0, has_side_effects=True, vmem_limit_bytes=60 * 1024 * 1024
            ),
        )(positions, wavelet, traces, src_now, src_prev, rec_now, rec_prev, courant_sq)

    placed = (
        P(("groups", "shot"), "gx", None, None),
        P(("groups", "shot"), "gx", None, None),
        P(("groups", "shot"), "gx", None, None),
        P(("groups", "shot"), "gx", None, None),
        P(("groups", "gx"), None, None),
        P(("groups", "shot"), None),
        P(("groups", "shot"), None, "gx"),
        P(("groups", "shot"), None),
    )
    return jax.shard_map(
        local,
        mesh=mesh,
        in_specs=placed,
        out_specs=P(("groups", "shot"), "gx", None, None),
        check_vma=False,
    )
```
